128 devices in a mesh: dp: 16 (over z, x), tensor: 8 (over y, core).
Axes of the slice: x: 4, y: 4, z: 4, core: 2. Of those that a mesh axis runs over, the one named last changes fastest.
Arguments:
- tokens: bfloat16 [128, 128, 8192], P('dp', None, 'tensor'), may hold values from -6 to 6
- shared_prefix_tokens: bfloat16 [16, 256, 8192], P('dp', None, 'tensor'), may hold values from -6 to 6
- input_norm_gain: bfloat16 [8192], replicated, may hold values from 0.5 to 8
- query_weight: bfloat16 [8192, 8192], P(None, 'tensor'), may hold values from -0.0625 to 0.0625
- key_weight: bfloat16 [8192, 1024], P(None, 'tensor'), may hold values from -0.0625 to 0.0625
- value_weight: bfloat16 [8192, 1024], P(None, 'tensor'), may hold values from -0.0625 to 0.0625
- adapter_down_weight: bfloat16 [64, 8192, 16], P('dp', 'tensor'), may hold values from -0.0625 to 0.0625
- adapter_up_weight: bfloat16 [64, 16, 8192], P('dp', None, 'tensor'), may hold values from -0.75 to 0.75
- adapter_position: int32 [64], replicated, may hold values from 0 to 63, as said below
- request_adapter: int32 [128], P('dp'), may hold values from 0 to 63, as said below
- request_group: int32 [128], P('dp'), may hold values from 0 to 15
- lengths: int32 [128], P('dp'), may hold values from 1 to 128
- request_page_table: int32 [128, 1], P('dp'), may hold values from 0 to 127, as said below
Outputs:
- context: bfloat16 [128, 128, 8192], P('dp', None, 'tensor')
- paged_key_values: bfloat16 [128, 2, 128, 1024], P('dp', None, None, 'tensor')
The draws below stay inside these ranges and needn't reach their ends.
Inputs may be any that keep to these rules, and one draw needn't show every extreme that they name: A permutation: adapter a is held at slot adapter_position[a], on index adapter_position[a] // 4 of dp. `request_adapter`: the 8 requests of one index of dp use adapters held by 8 different indices of dp. `request_page_table`: the requests of index i of dp use the pages i * 8 to (i + 1) * 8 - 1, each page once.
All inputs are finite; a program needn't handle non-finite values.
Results may differ from the reference program's by a relative error of at most 0.011.
The reference program's roundings to bfloat16 on the way count: a program that leaves them out, or rounds other values in their place, can miss the bound.
Values may be sent and summed in bfloat16 or wider, within the bound.
No kernel may reach another device: no remote copies, remote signals or barrier semaphores. Data moves between devices by JAX's collectives and lax.ppermute only.
A program may use at most 128 MiB of HBM per device.

```python
import math
import jax
import jax.numpy as jnp
import numpy as np
from jax import lax

MODEL_WIDTH = 8192
QUERY_HEADS = 64
KEY_VALUE_HEADS = 8
HEAD_WIDTH = 128
ADAPTER_RANK = 16
ADP_DEV = 4
ADAPTER_COUNT = 64
PAGE_TOKENS = 128
REQUEST_PAGES = 1
REQUEST_LENGTH = 128
REQ_DEV = 8
REQUEST_COUNT = 128
PREFIX_LENGTH = 256
GROUPS = 16
PAGE_COUNT = 128
N_DP = 16


def routing(key):
    base = jax.random.fold_in(key, 7)
    key_rows = jax.random.split(base, 4)
    slots = jax.random.permutation(key_rows[0], ADAPTER_COUNT).astype(jnp.int32)
    hot = jax.random.randint(key_rows[1], (), 0, N_DP)

    def device_offsets(dkey):
        first, second = jax.random.split(dkey)
        others = jax.random.permutation(first, N_DP - 1)[:REQ_DEV - 1] + 1
        offsets = jnp.concatenate([jnp.zeros((1,), jnp.int32), others.astype(jnp.int32)])
        return jax.random.permutation(second, offsets)
    offsets = jax.vmap(device_offsets)(jax.random.split(key_rows[2], N_DP))
    owners = (hot + offsets) % N_DP
    local = jax.random.randint(key_rows[3], (N_DP, REQ_DEV), 0, ADP_DEV)
    held = owners * ADP_DEV + local
    inverse = jnp.argsort(slots)
    chosen = inverse[held.reshape(-1)].astype(jnp.int32)
    return (slots, chosen)


def draw_adapter_position(key, part):
    return routing(key)[0]


def draw_request_adapter(key, part):
    return routing(key)[1]


def draw_lengths(key, part):
    first, second = jax.random.split(jax.random.fold_in(key, 11))
    values = jax.random.randint(first, (REQUEST_COUNT,), 1, REQUEST_LENGTH + 1)
    full = jax.random.randint(second, (), 0, REQUEST_COUNT)
    return jnp.where(jnp.arange(REQUEST_COUNT) == full, REQUEST_LENGTH, values).astype(jnp.int32)


def draw_request_page_table(key, part):
    pool = REQ_DEV * REQUEST_PAGES
    key_rows = jax.random.split(jax.random.fold_in(key, 13), N_DP)
    perms = jax.vmap(lambda k: jax.random.permutation(k, pool))(key_rows)
    pages = perms + (jnp.arange(N_DP) * pool)[:, None]
    return pages.reshape(REQUEST_COUNT, REQUEST_PAGES).astype(jnp.int32)


def draw_input_norm_gain(key, part):
    inner = jax.random.fold_in(key, 17)
    values = jax.random.uniform(inner, (MODEL_WIDTH,), jnp.float32, 0.5, 1.5)
    return values.astype(jnp.bfloat16)


def with_ends(result, own_key, smallest, top_value):
    dims = result.shape
    spot = [jax.random.randint(jax.random.fold_in(own_key, axis), (), 0, dims[axis]) for axis in range(len(dims))]
    result = result.at[tuple(spot)].set(smallest)
    longest = dims.index(max(dims))
    spot[longest] = (spot[longest] + 1) % dims[longest]
    return result.at[tuple(spot)].set(top_value)


def block_scale(rng, extent, cuts, least, top_value):
    level, own = 1.0, jax.random.fold_in(rng, 6)
    for axis_at, shards_of in cuts:
        steps = jnp.exp(jax.random.uniform(jax.random.fold_in(own, axis_at), (shards_of,), jnp.float32, least / len(cuts), top_value / len(cuts)))
        level = level * jnp.repeat(steps, extent[axis_at] // shards_of).reshape([-1 if axis == axis_at else 1 for axis in range(len(extent))])
    return level


def rank_table(number_of, slope):
    portions = [(1 << 20) // math.isqrt(rank ** slope) + 1 for rank in range(1, number_of + 1)]
    spread = 1 + sum(portions) // (1 << 30)
    return np.cumsum(np.array([max(1, weight // spread) for weight in portions]))


def ranked_ids(key, dims, amount, slope):
    listing = rank_table(amount, slope)
    lot = jax.random.randint(jax.random.fold_in(key, 1), dims, 0, int(listing[amount - 1]))
    standing = jnp.searchsorted(jnp.asarray(listing, jnp.int32), lot, side="right")
    return jax.random.permutation(jax.random.fold_in(key, 2), amount)[standing].astype(jnp.int32)


def scatter_about(stream_key, shape, deviation, reach, shards=(), kind=jnp.bfloat16):
    values = deviation * jax.random.normal(stream_key, shape, jnp.float32)
    if shards:
        values = values * block_scale(stream_key, shape, shards, -0.22, 0.18)
    return jnp.clip(values, -reach, reach).astype(kind)


def setup_inputs(seed: int = 0) -> dict:
    arg_keys = jax.random.split(jax.random.key(seed), 14)
    return {
        "tokens": scatter_about(arg_keys[0], (REQUEST_COUNT, REQUEST_LENGTH, MODEL_WIDTH), 1.0, 6.0, ((0, 16), (2, 8))),
        "shared_prefix_tokens": scatter_about(arg_keys[1], (GROUPS, PREFIX_LENGTH, MODEL_WIDTH), 1.0, 6.0, ((0, 16), (2, 8))),
        "input_norm_gain": draw_input_norm_gain(jax.random.fold_in(arg_keys[13], 71), 0),
        "query_weight": scatter_about(arg_keys[3], (MODEL_WIDTH, QUERY_HEADS * HEAD_WIDTH), MODEL_WIDTH ** -0.5, 0.0625, ((1, 8),)),
        "key_weight": scatter_about(arg_keys[4], (MODEL_WIDTH, KEY_VALUE_HEADS * HEAD_WIDTH), MODEL_WIDTH ** -0.5, 0.0625, ((1, 8),)),
        "value_weight": scatter_about(arg_keys[5], (MODEL_WIDTH, KEY_VALUE_HEADS * HEAD_WIDTH), MODEL_WIDTH ** -0.5, 0.0625, ((1, 8),)),
        "adapter_down_weight": scatter_about(arg_keys[6], (ADAPTER_COUNT, MODEL_WIDTH, ADAPTER_RANK), MODEL_WIDTH ** -0.5, 0.0625, ((0, 16), (1, 8))),
        "adapter_up_weight": scatter_about(arg_keys[7], (ADAPTER_COUNT, ADAPTER_RANK, QUERY_HEADS * HEAD_WIDTH), (4 * ADAPTER_RANK) ** -0.5, 0.75, ((0, 16), (2, 8))),
        "adapter_position": draw_adapter_position(jax.random.fold_in(arg_keys[13], 71), 0),
        "request_adapter": draw_request_adapter(jax.random.fold_in(arg_keys[13], 71), 0),
        "request_group": with_ends(ranked_ids(arg_keys[10], (REQUEST_COUNT,), GROUPS, 2), jax.random.fold_in(arg_keys[10], 3), 0, GROUPS - 1).astype(jnp.int32),
        "lengths": draw_lengths(jax.random.fold_in(arg_keys[13], 71), 0),
        "request_page_table": draw_request_page_table(jax.random.fold_in(arg_keys[13], 71), 0),
    }


EPS = 1e-05
THETA = 500000.0
ADAPTER_SCALE = 2.0

def rope_tables(positions, width):
    half = width // 2
    freq = THETA ** (-(jnp.arange(half, dtype=jnp.float32) * 2.0 / width))
    angle = positions.astype(jnp.float32)[:, None] * freq[None, :]
    return (jnp.cos(angle), jnp.sin(angle))

def apply_rope(values, cosine, sine):
    half = values.shape[-1] // 2
    first = values[..., :half]
    second = values[..., half:]
    cos_b = cosine[:, None, :]
    sin_b = sine[:, None, :]
    return jnp.concatenate([first * cos_b - second * sin_b, second * cos_b + first * sin_b], axis=-1)

def normalize(rows, gain):
    values = rows.astype(jnp.float32)
    scale = lax.rsqrt(lax.optimization_barrier(jnp.mean(values * values, axis=-1, keepdims=True)) + EPS)
    return (values * scale * gain.astype(jnp.float32)).astype(jnp.bfloat16)

def reference(tokens, shared_prefix_tokens, input_norm_gain, query_weight, key_weight, value_weight, adapter_down_weight, adapter_up_weight, adapter_position, request_adapter, request_group, lengths, request_page_table):
    group_members = QUERY_HEADS // KEY_VALUE_HEADS
    pre_cos, pre_sin = rope_tables(jnp.arange(PREFIX_LENGTH), HEAD_WIDTH)
    own_cos, own_sin = rope_tables(PREFIX_LENGTH + jnp.arange(REQUEST_LENGTH), HEAD_WIDTH)

    def prefix_pair(rows):
        normalized_rows = normalize(rows, input_norm_gain)
        key_rows = jnp.dot(normalized_rows, key_weight, preferred_element_type=jnp.float32).reshape(PREFIX_LENGTH, KEY_VALUE_HEADS, HEAD_WIDTH)
        value_rows = jnp.dot(normalized_rows, value_weight, preferred_element_type=jnp.float32).reshape(PREFIX_LENGTH, KEY_VALUE_HEADS, HEAD_WIDTH)
        return (apply_rope(key_rows, pre_cos, pre_sin).astype(jnp.bfloat16), value_rows.astype(jnp.bfloat16))
    pre_keys, pre_vals = lax.map(prefix_pair, shared_prefix_tokens)
    slots = adapter_position[request_adapter].astype(jnp.int32)
    seen = jnp.arange(PREFIX_LENGTH + REQUEST_LENGTH)[None, :]
    rows_at = jnp.arange(REQUEST_LENGTH)[:, None]
    allowed = (seen < PREFIX_LENGTH) | (seen - PREFIX_LENGTH <= rows_at)

    def one_request(item):
        rows, adapter_slot_index, group, length = item
        normed_input = normalize(rows, input_norm_gain)
        down_matrix = lax.dynamic_index_in_dim(adapter_down_weight, adapter_slot_index, 0, keepdims=False)
        up_matrix = lax.dynamic_index_in_dim(adapter_up_weight, adapter_slot_index, 0, keepdims=False)
        low_rank_rows = jnp.dot(normed_input, down_matrix, preferred_element_type=jnp.float32).astype(jnp.bfloat16)
        adapter_delta = (ADAPTER_SCALE * jnp.dot(low_rank_rows, up_matrix, preferred_element_type=jnp.float32)).astype(jnp.bfloat16)
        query_rows = jnp.dot(normed_input, query_weight, preferred_element_type=jnp.float32) + adapter_delta.astype(jnp.float32)
        query_rows = apply_rope(query_rows.reshape(REQUEST_LENGTH, QUERY_HEADS, HEAD_WIDTH), own_cos, own_sin).astype(jnp.bfloat16)
        key_rows = jnp.dot(normed_input, key_weight, preferred_element_type=jnp.float32).reshape(REQUEST_LENGTH, KEY_VALUE_HEADS, HEAD_WIDTH)
        key_rows = apply_rope(key_rows, own_cos, own_sin).astype(jnp.bfloat16)
        value_rows = jnp.dot(normed_input, value_weight, preferred_element_type=jnp.float32).reshape(REQUEST_LENGTH, KEY_VALUE_HEADS, HEAD_WIDTH).astype(jnp.bfloat16)
        live = jnp.arange(REQUEST_LENGTH) < length
        key_rows = jnp.where(live[:, None, None], key_rows, jnp.zeros_like(key_rows))
        value_rows = jnp.where(live[:, None, None], value_rows, jnp.zeros_like(value_rows))
        all_keys = jnp.concatenate([lax.dynamic_index_in_dim(pre_keys, group, 0, keepdims=False), key_rows], 0)
        all_vals = jnp.concatenate([lax.dynamic_index_in_dim(pre_vals, group, 0, keepdims=False), value_rows], 0)
        grouped_query = query_rows.reshape(REQUEST_LENGTH, KEY_VALUE_HEADS, group_members, HEAD_WIDTH).astype(jnp.float32)
        scores = jnp.einsum('tkgd,skd->kgts', grouped_query, all_keys.astype(jnp.float32)) * HEAD_WIDTH ** (-0.5)
        scores = jnp.where(allowed[None, None], scores, -1e+30)
        top = lax.optimization_barrier(jnp.max(scores, axis=-1, keepdims=True))
        weights = jnp.exp(scores - top)
        probs = (weights / lax.optimization_barrier(jnp.sum(weights, axis=-1, keepdims=True))).astype(jnp.bfloat16)
        attention_output = jnp.einsum('kgts,skd->tkgd', probs.astype(jnp.float32), all_vals.astype(jnp.float32))
        attention_output = jnp.where(live[:, None, None, None], attention_output, 0.0).reshape(REQUEST_LENGTH, QUERY_HEADS * HEAD_WIDTH).astype(jnp.bfloat16)
        return (attention_output, key_rows.reshape(REQUEST_LENGTH, KEY_VALUE_HEADS * HEAD_WIDTH), value_rows.reshape(REQUEST_LENGTH, KEY_VALUE_HEADS * HEAD_WIDTH))
    context, key_rows, value_rows = lax.map(one_request, (tokens, slots, request_group.astype(jnp.int32), lengths.astype(jnp.int32)))
    page_blocks = jnp.stack([key_rows.reshape(REQUEST_COUNT, REQUEST_PAGES, PAGE_TOKENS, KEY_VALUE_HEADS * HEAD_WIDTH), value_rows.reshape(REQUEST_COUNT, REQUEST_PAGES, PAGE_TOKENS, KEY_VALUE_HEADS * HEAD_WIDTH)], 2)
    page_blocks = page_blocks.reshape(REQUEST_COUNT * REQUEST_PAGES, 2, PAGE_TOKENS, KEY_VALUE_HEADS * HEAD_WIDTH)
    paged_key_values = jnp.zeros((PAGE_COUNT, 2, PAGE_TOKENS, KEY_VALUE_HEADS * HEAD_WIDTH), jnp.bfloat16).at[request_page_table.reshape(-1)].set(page_blocks)
    return (context, paged_key_values)
```

```python
import functools

import jax
import jax.numpy as jnp
import numpy as np
from jax import lax
from jax.experimental import pallas as pl
from jax.experimental.pallas import tpu as pltpu
from jax.sharding import PartitionSpec as P

HEAD_WIDTH = 128
RANK = 16
EPS = 1e-05
THETA = 500000.0
ADAPTER_SCALE = 2.0
F32 = jnp.float32
BF16 = jnp.bfloat16
CHUNKS = (2, 2, 2, 2)

SWAP = [(y * 2 + c, y * 2 + 1 - c) for y in range(4) for c in range(2)]
RING = [(y * 2 + c, (y + 1 - 2 * c) % 4 * 2 + c) for y in range(4) for c in range(2)]
BACK = [(y * 2 + c, (y - 1 + 2 * c) % 4 * 2 + c) for y in range(4) for c in range(2)]


def plane_shift(k, stage):
    pairs = []
    for z in range(4):
        for x in range(4):
            for t in range(8):
                along_x = (t % 2 == 0) == (stage == 0)
                to_z, to_x = (z, (x + k) % 4) if along_x else ((z + k) % 4, x)
                pairs.append(((z * 4 + x) * 8 + t, (to_z * 4 + to_x) * 8 + t))
    return pairs


def over_tensor(value, pairs):
    return lax.ppermute(value, "tensor", pairs)


def over_plane(value, stage):
    send = lambda k: lax.ppermute(value, ("dp", "tensor"), plane_shift(k, stage))
    return [value, send(-1), send(2), send(1)]


def gather_plane(value):
    first = jnp.stack(over_plane(value, 0))
    return over_plane(first, 1)


def rotate_tables(start, count):
    half = HEAD_WIDTH // 2
    freq = THETA ** (-(np.arange(half) * 2.0 / HEAD_WIDTH))
    angle = np.arange(start, start + count)[:, None] * freq[None, :]
    cosine, sine = np.cos(angle), np.sin(angle)
    return (
        np.concatenate([cosine, cosine], 1).astype(np.float32),
        np.concatenate([-sine, sine], 1).astype(np.float32),
    )


def rotate(value, cosine, sine):
    return value * cosine + pltpu.roll(value, HEAD_WIDTH // 2, 1) * sine


def dot(a, b, dims=((1,), (0,))):
    return lax.dot_general(a, b, (dims, ((), ())), preferred_element_type=F32)


def norm_kernel(place, own, other, scale, gain_own, gain_other, out):
    for r in range(own.shape[0]):
        row = jnp.broadcast_to(scale[r], (128, 128))
        eye = lax.broadcasted_iota(jnp.int32, (128, 128), 0) == lax.broadcasted_iota(
            jnp.int32, (128, 128), 1
        )
        column = jnp.sum(jnp.where(eye, row, 0.0), axis=1, keepdims=True)
        out[0, r] = (own[r].astype(F32) * column * gain_own[0]).astype(BF16)
        out[1, r] = (other[r].astype(F32) * column * gain_other[0]).astype(BF16)


def norm_call(first, count, gain_ids, own, other, scale, gain):
    _, seq, part = own.shape
    rows = lambda i, ids: (first + i, 0, 0)
    return pl.pallas_call(
        norm_kernel,
        out_shape=jax.ShapeDtypeStruct((2, count, seq, part), BF16),
        grid_spec=pltpu.PrefetchScalarGridSpec(
            num_scalar_prefetch=1,
            grid=(count,),
            in_specs=[
                pl.BlockSpec((1, seq, part), rows),
                pl.BlockSpec((1, seq, part), rows),
                pl.BlockSpec((1, 1, seq), rows),
                pl.BlockSpec((1, 1, part), lambda i, ids: (ids[0], 0, 0)),
                pl.BlockSpec((1, 1, part), lambda i, ids: (ids[1], 0, 0)),
            ],
            out_specs=pl.BlockSpec((2, 1, seq, part), lambda i, ids: (0, i, 0, 0)),
        ),
        name="norm",
    )(gain_ids, own, other, scale, gain, gain)


def prefix_kernel(order, mine, near, cross, far, far_cross, gain, kw, vw, cosine, sine, out):
    width = mine.shape[-1]
    pieces = [mine[0], mine[1], near[0], near[1], cross[0], cross[1], far[...], far_cross[...]]
    total = jnp.zeros((mine.shape[1], 1), F32)
    for piece in pieces:
        value = piece.astype(F32)
        total = total + jnp.sum(value * value, axis=1, keepdims=True)
    scale = lax.rsqrt(total * (1.0 / (8 * width)) + EPS)
    acc = jnp.zeros((mine.shape[1], 2 * HEAD_WIDTH), F32)
    for i, piece in enumerate(pieces):
        block = order[i]
        at = pl.ds(pl.multiple_of(block * width, width), width)
        weight = jnp.concatenate([kw[at, :], vw[at, :]], axis=1)
        normed = (piece.astype(F32) * scale * gain[block]).astype(BF16)
        acc = acc + dot(normed, weight)
    out[0] = rotate(acc[:, :HEAD_WIDTH], cosine[...], sine[...]).astype(BF16)
    out[1] = acc[:, HEAD_WIDTH:].astype(BF16)


def prefix_call(order, mine, near, cross, far, far_cross, gain, kw, vw, cosine, sine):
    rows = mine.shape[1]
    full = pl.BlockSpec(memory_space=pltpu.VMEM)
    return pl.pallas_call(
        prefix_kernel,
        out_shape=jax.ShapeDtypeStruct((2, rows, HEAD_WIDTH), BF16),
        in_specs=[pl.BlockSpec(memory_space=pltpu.SMEM)] + [full] * 10,
        out_specs=full,
        name="prefix",
    )(order, mine, near, cross, far, far_cross, gain, kw, vw, cosine, sine)


def pick_copies(sources, select, first, second, target, sem, act):
    for j, source in enumerate(sources):

        @pl.when(select == j)
        def _(source=source):
            act(pltpu.make_async_copy(source.at[first] if second is None else source.at[first, second], target, sem))


def low_kernel(pick, x0, x1, x2, x3, a0, a1, a2, a3, part, up, held, sems):
    for r in range(held.shape[0]):
        pick_copies(
            (a0, a1, a2, a3), pick[r, 0], pick[r, 1], pick[r, 2], held.at[r], sems.at[r], lambda c: c.start()
        )
    r = 0
    for x in (x0, x1, x2, x3):
        for i in range(x.shape[1]):
            pltpu.make_async_copy(a0.at[0, 0], held.at[r], sems.at[r]).wait()
            part[r] = dot(held[r, :RANK], x[0, i], ((1,), (1,)))
            up[r] = held[r, RANK:]
            r += 1


def low_call(pick, chunks, adapters):
    requests = pick.shape[0]
    seq, part = chunks[0].shape[2:]
    full = pl.BlockSpec(memory_space=pltpu.VMEM)
    some = [pl.BlockSpec((1,) + c.shape[1:], lambda i, *_: (0, 0, 0, 0)) for c in chunks]
    return pl.pallas_call(
        low_kernel,
        out_shape=(
            jax.ShapeDtypeStruct((requests, RANK, seq), F32),
            jax.ShapeDtypeStruct((requests, RANK, part), BF16),
        ),
        grid_spec=pltpu.PrefetchScalarGridSpec(
            num_scalar_prefetch=1,
            grid=(1,),
            in_specs=some + [pl.BlockSpec(memory_space=pl.ANY)] * 4,
            out_specs=[
                pl.BlockSpec((requests, RANK, seq), lambda i, *_: (0, 0, 0)),
                pl.BlockSpec((requests, RANK, part), lambda i, *_: (0, 0, 0)),
            ],
            scratch_shapes=[
                pltpu.VMEM((requests, 2 * RANK, part), BF16),
                pltpu.SemaphoreType.DMA((requests,)),
            ],
        ),
        name="low",
    )(pick, *chunks, *adapters)


def block_kernel(
    first,
    count,
    order,
    table,
    mine,
    near,
    cross,
    far,
    far_cross,
    qw,
    kw,
    vw,
    low,
    up,
    cosine,
    sine,
    p0,
    p1,
    p2,
    p3,
    *rest,
):
    context, pages, xs, acc_q, acc_kv, pairs, page, x_sem, pair_sem, page_sem = rest[-10:]
    k = pl.program_id(0)
    seq, width = xs.shape[2:]
    pre = pairs.shape[2]
    sources = [mine.at[0], mine.at[1], near.at[0], near.at[1], cross.at[0], cross.at[1], far, far_cross]

    @pl.when(k == 0)
    def _():
        for i, source in enumerate(sources):
            pltpu.make_async_copy(source, xs.at[i], x_sem.at[i]).start()
        for r in range(count):
            pick_copies(
                (p0, p1, p2, p3),
                table[first + r, 0],
                table[first + r, 1],
                None,
                pairs.at[r],
                pair_sem.at[r],
                lambda c: c.start(),
            )

    pltpu.make_async_copy(far, xs.at[k], x_sem.at[k]).wait()
    x = xs[k].reshape(count * seq, width)
    part_q = dot(x, qw[...])
    part_kv = dot(x, jnp.concatenate([kw[...], vw[...]], axis=1))

    @pl.when(k == 0)
    def _():
        acc_q[...] = part_q
        acc_kv[...] = part_kv

    @pl.when(k > 0)
    def _():
        acc_q[...] += part_q
        acc_kv[...] += part_kv

    @pl.when(k == pl.num_programs(0) - 1)
    def _():
        heads = acc_q.shape[1] // HEAD_WIDTH
        cos_t, sin_t = cosine[...], sine[...]
        token = lax.broadcasted_iota(jnp.int32, (seq, HEAD_WIDTH), 0)
        causal = lax.broadcasted_iota(jnp.int32, (seq, seq), 1) <= lax.broadcasted_iota(
            jnp.int32, (seq, seq), 0
        )
        allowed = jnp.concatenate([jnp.ones((seq, pre), jnp.bool_), causal], axis=1)
        for r in range(count):
            pltpu.make_async_copy(p0.at[0], pairs.at[r], pair_sem.at[r]).wait()
            live = token < table[first + r, 2]
            rows = slice(r * seq, (r + 1) * seq)
            key = rotate(acc_kv[rows, :HEAD_WIDTH], cos_t, sin_t)
            key = jnp.where(live, key, 0.0).astype(BF16)
            value = jnp.where(live, acc_kv[rows, HEAD_WIDTH:], 0.0).astype(BF16)
            page[r, 0] = key
            page[r, 1] = value
            pltpu.make_async_copy(page.at[r], pages.at[table[first + r, 3]], page_sem.at[r]).start()
            keys = jnp.concatenate([pairs[r, 0], key], axis=0)
            values = jnp.concatenate([pairs[r, 1], value], axis=0)
            delta = ADAPTER_SCALE * dot(low[first + r], up[first + r], ((0,), (0,)))
            query = acc_q[rows, :] + delta.astype(BF16).astype(F32)
            for h in range(heads):
                lanes = slice(h * HEAD_WIDTH, (h + 1) * HEAD_WIDTH)
                q = rotate(query[:, lanes], cos_t, sin_t).astype(BF16)
                scores = dot(q, keys, ((1,), (1,))) * (HEAD_WIDTH**-0.5)
                scores = jnp.where(allowed, scores, -1e30)
                top = jnp.max(scores, axis=1, keepdims=True)
                weights = jnp.exp(scores - top)
                inverse = 1.0 / jnp.sum(weights, axis=1, keepdims=True)
                probs = (weights * inverse).astype(BF16)
                out = dot(probs, values)
                context[r, :, lanes] = jnp.where(live, out, 0.0).astype(BF16)
        for r in range(count):
            pltpu.make_async_copy(page.at[r], pages.at[0], page_sem.at[r]).wait()


def block_call(first, count, requests, order, table, x, weights, low, up, tables, pairs, before):
    seq, width = x[0].shape[2:]
    q_width = weights[0].shape[1]
    pre = pairs[0].shape[2]
    hbm = pl.BlockSpec(memory_space=pl.ANY)
    whole = lambda a: pl.BlockSpec(a.shape, lambda k, *_: (0,) * a.ndim)
    weight = lambda a: pl.BlockSpec((width, a.shape[1]), lambda k, order, table: (order[k], 0))
    operands = [*x, *weights, low, up, *tables, *pairs, *before]
    specs = (
        [hbm] * 5
        + [weight(w) for w in weights]
        + [whole(low), whole(up)]
        + [whole(t) for t in tables]
        + [hbm] * (4 + len(before))
    )
    at = len(operands)
    aliases = {at: 0, at + 1: 1} if before else {}
    return pl.pallas_call(
        functools.partial(block_kernel, first, count),
        out_shape=(
            jax.ShapeDtypeStruct((requests, seq, q_width), BF16),
            jax.ShapeDtypeStruct((requests, 2, seq, HEAD_WIDTH), BF16),
        ),
        grid_spec=pltpu.PrefetchScalarGridSpec(
            num_scalar_prefetch=2,
            grid=(8,),
            in_specs=specs,
            out_specs=[pl.BlockSpec((count, seq, q_width), lambda k, *_: (first // count, 0, 0)), hbm],
            scratch_shapes=[
                pltpu.VMEM((8, count, seq, width), BF16),
                pltpu.VMEM((count * seq, q_width), F32),
                pltpu.VMEM((count * seq, 2 * HEAD_WIDTH), F32),
                pltpu.VMEM((count, 2, pre, HEAD_WIDTH), BF16),
                pltpu.VMEM((count, 2, seq, HEAD_WIDTH), BF16),
                pltpu.SemaphoreType.DMA((8,)),
                pltpu.SemaphoreType.DMA((count,)),
                pltpu.SemaphoreType.DMA((count,)),
            ],
        ),
        input_output_aliases=aliases,
        name="block",
    )(order, table, *operands)


def ring_rest(mine):
    near = over_tensor(mine, RING)
    far = over_tensor(near[0], RING)
    cross = over_tensor(near, SWAP)
    far_cross = over_tensor(far, SWAP)
    return near, cross, far, far_cross


def on_device(
    tokens,
    shared_prefix_tokens,
    input_norm_gain,
    query_weight,
    key_weight,
    value_weight,
    adapter_down_weight,
    adapter_up_weight,
    adapter_position,
    request_adapter,
    request_group,
    lengths,
    request_page_table,
):
    requests, seq, part = tokens.shape
    pre = shared_prefix_tokens.shape[1]
    held = adapter_up_weight.shape[0]
    column = lax.axis_index("tensor")
    place = lax.axis_index("dp")
    core = column % 2
    y = column // 2
    z_at, x_at = place // 4, place % 4

    near_y = (y + 3 + 2 * core) % 4
    cross_y = (y + 1 + 2 * core) % 4
    far_y = (y + 2) % 4
    order = jnp.stack(
        [
            column,
            column ^ 1,
            near_y * 2 + core,
            near_y * 2 + 1 - core,
            cross_y * 2 + 1 - core,
            cross_y * 2 + core,
            far_y * 2 + core,
            far_y * 2 + 1 - core,
        ]
    ).astype(jnp.int32)

    def relative(owner):
        dz, dx = (owner // 4 - z_at) % 4, (owner % 4 - x_at) % 4
        return jnp.where(core == 0, dx, dz), jnp.where(core == 0, dz, dx)

    prefix = shared_prefix_tokens.reshape(pre, part)
    prefix_other = over_tensor(prefix, SWAP)
    tokens_other = over_tensor(tokens, SWAP)
    adapters = gather_plane(
        jnp.concatenate([adapter_down_weight.transpose(0, 2, 1), adapter_up_weight], axis=1)
    )
    prefix_mine = jnp.stack([prefix, prefix_other])
    prefix_rest = ring_rest(prefix_mine)

    square = lambda v: jnp.sum(jnp.square(v.astype(F32)), axis=-1)
    chip = square(tokens) + square(tokens_other)
    one = over_tensor(chip, BACK)
    two = over_tensor(one, BACK)
    mean = (chip + two + one + over_tensor(one, SWAP)) * (1.0 / (8 * part))
    scale = lax.rsqrt(mean + EPS).reshape(requests, 1, seq)

    gain = input_norm_gain.astype(F32).reshape(8, 1, part)
    firsts = [sum(CHUNKS[:i]) for i in range(len(CHUNKS))]
    chunks = [
        norm_call(f, n, order[:2], tokens, tokens_other, scale, gain)
        for f, n in zip(firsts, CHUNKS)
    ]
    gathered = [(c,) + ring_rest(c) for c in chunks]

    pre_cos, pre_sin = rotate_tables(0, pre)
    pair = prefix_call(
        order, prefix_mine, *prefix_rest, gain, key_weight, value_weight, pre_cos, pre_sin
    )
    pairs = gather_plane(pair)

    ids = jnp.arange(adapter_position.shape[0])
    slots = jnp.sum(
        jnp.where(request_adapter[:, None] == ids[None, :], adapter_position[None, :], 0), axis=1
    )
    slot_1, slot_2 = relative(slots // held)
    pick = jnp.stack([slot_2, slot_1, slots % held], axis=1).astype(jnp.int32)
    part_low, up = low_call(pick, chunks, adapters)
    chip_low = part_low + over_tensor(part_low, SWAP)
    one_low = over_tensor(chip_low, BACK)
    two_low = over_tensor(one_low, BACK)
    low = (chip_low + two_low + one_low + over_tensor(one_low, SWAP)).astype(BF16)

    group_1, group_2 = relative(request_group)
    page = request_page_table.reshape(-1) - place * requests
    table = jnp.stack([group_2, group_1, lengths, page], axis=1).astype(jnp.int32)
    tables = rotate_tables(pre, seq)
    outs = ()
    for f, n, x in zip(firsts, CHUNKS, gathered):
        outs = block_call(
            f,
            n,
            requests,
            order,
            table,
            x,
            (query_weight, key_weight, value_weight),
            low,
            up,
            tables,
            pairs,
            outs,
        )
    return outs


def solution(mesh):
    in_specs = (
        P("dp", None, "tensor"),
        P("dp", None, "tensor"),
        P(),
        P(None, "tensor"),
        P(None, "tensor"),
        P(None, "tensor"),
        P("dp", "tensor", None),
        P("dp", None, "tensor"),
        P(),
        P("dp"),
        P("dp"),
        P("dp"),
        P("dp", None),
    )
    out_specs = (P("dp", None, "tensor"), P("dp", None, None, "tensor"))
    return jax.shard_map(
        on_device, mesh=mesh, in_specs=in_specs, out_specs=out_specs, check_vma=False
    )
```

```python
import functools

import jax
import jax.numpy as jnp
import numpy as np
from jax import lax
from jax.experimental import pallas as pl
from jax.experimental.pallas import tpu as pltpu
from jax.sharding import PartitionSpec as P

HEAD_WIDTH = 128
RANK = 16
EPS = 1e-05
THETA = 500000.0
ADAPTER_SCALE = 2.0
F32 = jnp.float32
BF16 = jnp.bfloat16
CHUNKS = (4, 4)
BLOCKS = ((0, 0, 2), (0, 2, 2), (1, 0, 4))

SWAP = [(y * 2 + c, y * 2 + 1 - c) for y in range(4) for c in range(2)]
RING = [(y * 2 + c, (y + 1 - 2 * c) % 4 * 2 + c) for y in range(4) for c in range(2)]
BACK = [(y * 2 + c, (y - 1 + 2 * c) % 4 * 2 + c) for y in range(4) for c in range(2)]


def plane_shift(k, stage):
    pairs = []
    for z in range(4):
        for x in range(4):
            for t in range(8):
                along_x = (t % 2 == 0) == (stage == 0)
                to_z, to_x = (z, (x + k) % 4) if along_x else ((z + k) % 4, x)
                pairs.append(((z * 4 + x) * 8 + t, (to_z * 4 + to_x) * 8 + t))
    return pairs


def over_tensor(value, pairs):
    return lax.ppermute(value, "tensor", pairs)


def over_plane(value, stage):
    send = lambda k: lax.ppermute(value, ("dp", "tensor"), plane_shift(k, stage))
    return [value, send(-1), send(2), send(1)]


def gather_plane(value):
    first = jnp.stack(over_plane(value, 0))
    return over_plane(first, 1)


def rotate_tables(start, count):
    half = HEAD_WIDTH // 2
    freq = THETA ** (-(np.arange(half) * 2.0 / HEAD_WIDTH))
    angle = np.arange(start, start + count)[:, None] * freq[None, :]
    cosine, sine = np.cos(angle), np.sin(angle)
    return (
        np.concatenate([cosine, cosine], 1).astype(np.float32),
        np.concatenate([-sine, sine], 1).astype(np.float32),
    )


def rotate(value, cosine, sine):
    return value * cosine + pltpu.roll(value, HEAD_WIDTH // 2, 1) * sine


def dot(a, b, dims=((1,), (0,))):
    return lax.dot_general(a, b, (dims, ((), ())), preferred_element_type=F32)


def norm_kernel(place, own, other, scale, gain_own, gain_other, out):
    for r in range(own.shape[0]):
        row = jnp.broadcast_to(scale[r], (128, 128))
        eye = lax.broadcasted_iota(jnp.int32, (128, 128), 0) == lax.broadcasted_iota(
            jnp.int32, (128, 128), 1
        )
        column = jnp.sum(jnp.where(eye, row, 0.0), axis=1, keepdims=True)
        out[0, r] = (own[r].astype(F32) * column * gain_own[0]).astype(BF16)
        out[1, r] = (other[r].astype(F32) * column * gain_other[0]).astype(BF16)


def norm_call(first, count, gain_ids, own, other, scale, gain):
    _, seq, part = own.shape
    rows = lambda i, ids: (first + i, 0, 0)
    return pl.pallas_call(
        norm_kernel,
        out_shape=jax.ShapeDtypeStruct((2, count, seq, part), BF16),
        grid_spec=pltpu.PrefetchScalarGridSpec(
            num_scalar_prefetch=1,
            grid=(count,),
            in_specs=[
                pl.BlockSpec((1, seq, part), rows),
                pl.BlockSpec((1, seq, part), rows),
                pl.BlockSpec((1, 1, seq), rows),
                pl.BlockSpec((1, 1, part), lambda i, ids: (ids[0], 0, 0)),
                pl.BlockSpec((1, 1, part), lambda i, ids: (ids[1], 0, 0)),
            ],
            out_specs=pl.BlockSpec((2, 1, seq, part), lambda i, ids: (0, i, 0, 0)),
        ),
        name="norm",
    )(gain_ids, own, other, scale, gain, gain)


def prefix_kernel(order, mine, near, cross, far, far_cross, gain, kw, vw, cosine, sine, out):
    width = mine.shape[-1]
    pieces = [mine[0], mine[1], near[0], near[1], cross[0], cross[1], far[...], far_cross[...]]
    total = jnp.zeros((mine.shape[1], 1), F32)
    for piece in pieces:
        value = piece.astype(F32)
        total = total + jnp.sum(value * value, axis=1, keepdims=True)
    scale = lax.rsqrt(total * (1.0 / (8 * width)) + EPS)
    acc = jnp.zeros((mine.shape[1], 2 * HEAD_WIDTH), F32)
    for i, piece in enumerate(pieces):
        block = order[i]
        at = pl.ds(pl.multiple_of(block * width, width), width)
        weight = jnp.concatenate([kw[at, :], vw[at, :]], axis=1)
        normed = (piece.astype(F32) * scale * gain[block]).astype(BF16)
        acc = acc + dot(normed, weight)
    out[0] = rotate(acc[:, :HEAD_WIDTH], cosine[...], sine[...]).astype(BF16)
    out[1] = acc[:, HEAD_WIDTH:].astype(BF16)


def prefix_call(order, mine, near, cross, far, far_cross, gain, kw, vw, cosine, sine):
    rows = mine.shape[1]
    full = pl.BlockSpec(memory_space=pltpu.VMEM)
    return pl.pallas_call(
        prefix_kernel,
        out_shape=jax.ShapeDtypeStruct((2, rows, HEAD_WIDTH), BF16),
        in_specs=[pl.BlockSpec(memory_space=pltpu.SMEM)] + [full] * 10,
        out_specs=full,
        name="prefix",
    )(order, mine, near, cross, far, far_cross, gain, kw, vw, cosine, sine)


def pick_copies(sources, select, first, second, target, sem, act):
    for j, source in enumerate(sources):

        @pl.when(select == j)
        def _(source=source):
            act(pltpu.make_async_copy(source.at[first] if second is None else source.at[first, second], target, sem))


def low_kernel(pick, x0, x1, a0, a1, a2, a3, part, up, held, sems):
    for r in range(held.shape[0]):
        pick_copies(
            (a0, a1, a2, a3), pick[r, 0], pick[r, 1], pick[r, 2], held.at[r], sems.at[r], lambda c: c.start()
        )
    r = 0
    for x in (x0, x1):
        for i in range(x.shape[1]):
            pltpu.make_async_copy(a0.at[0, 0], held.at[r], sems.at[r]).wait()
            part[r] = dot(held[r, :RANK], x[0, i], ((1,), (1,)))
            up[r] = held[r, RANK:]
            r += 1


def low_call(pick, chunks, adapters):
    requests = pick.shape[0]
    seq, part = chunks[0].shape[2:]
    full = pl.BlockSpec(memory_space=pltpu.VMEM)
    some = [pl.BlockSpec((1,) + c.shape[1:], lambda i, *_: (0, 0, 0, 0)) for c in chunks]
    return pl.pallas_call(
        low_kernel,
        out_shape=(
            jax.ShapeDtypeStruct((requests, RANK, seq), F32),
            jax.ShapeDtypeStruct((requests, RANK, part), BF16),
        ),
        grid_spec=pltpu.PrefetchScalarGridSpec(
            num_scalar_prefetch=1,
            grid=(1,),
            in_specs=some + [pl.BlockSpec(memory_space=pl.ANY)] * 4,
            out_specs=[
                pl.BlockSpec((requests, RANK, seq), lambda i, *_: (0, 0, 0)),
                pl.BlockSpec((requests, RANK, part), lambda i, *_: (0, 0, 0)),
            ],
            scratch_shapes=[
                pltpu.VMEM((requests, 2 * RANK, part), BF16),
                pltpu.SemaphoreType.DMA((requests,)),
            ],
        ),
        name="low",
    )(pick, *chunks, *adapters)


def block_kernel(
    first,
    start,
    count,
    order,
    table,
    mine,
    near,
    cross,
    far,
    far_cross,
    qw,
    kw,
    vw,
    low,
    up,
    cosine,
    sine,
    p0,
    p1,
    p2,
    p3,
    *rest,
):
    context, pages, xs, acc_q, acc_kv, pairs, page, x_sem, pair_sem, page_sem = rest[-10:]
    k = pl.program_id(0)
    seq, width = xs.shape[2:]
    pre = pairs.shape[2]
    sources = [mine.at[0], mine.at[1], near.at[0], near.at[1], cross.at[0], cross.at[1], far, far_cross]

    @pl.when(k == 0)
    def _():
        for i, source in enumerate(sources):
            pltpu.make_async_copy(source.at[start : start + count], xs.at[i], x_sem.at[i]).start()
        for r in range(count):
            pick_copies(
                (p0, p1, p2, p3),
                table[first + r, 0],
                table[first + r, 1],
                None,
                pairs.at[r],
                pair_sem.at[r],
                lambda c: c.start(),
            )

    pltpu.make_async_copy(far.at[start : start + count], xs.at[k], x_sem.at[k]).wait()
    x = xs[k].reshape(count * seq, width)
    part_q = dot(x, qw[...])
    part_kv = dot(x, jnp.concatenate([kw[...], vw[...]], axis=1))

    @pl.when(k == 0)
    def _():
        acc_q[...] = part_q
        acc_kv[...] = part_kv

    @pl.when(k > 0)
    def _():
        acc_q[...] += part_q
        acc_kv[...] += part_kv

    @pl.when(k == pl.num_programs(0) - 1)
    def _():
        heads = acc_q.shape[1] // HEAD_WIDTH
        cos_t, sin_t = cosine[...], sine[...]
        token = lax.broadcasted_iota(jnp.int32, (seq, HEAD_WIDTH), 0)
        causal = lax.broadcasted_iota(jnp.int32, (seq, seq), 1) <= lax.broadcasted_iota(
            jnp.int32, (seq, seq), 0
        )
        allowed = jnp.concatenate([jnp.ones((seq, pre), jnp.bool_), causal], axis=1)

        def request(r, carry):
            pltpu.make_async_copy(p0.at[0], pairs.at[r], pair_sem.at[r]).wait()
            live = token < table[first + r, 2]
            rows = pl.ds(pl.multiple_of(r * seq, seq), seq)
            key = rotate(acc_kv[rows, :HEAD_WIDTH], cos_t, sin_t)
            key = jnp.where(live, key, 0.0).astype(BF16)
            value = jnp.where(live, acc_kv[rows, HEAD_WIDTH:], 0.0).astype(BF16)
            page[r, 0] = key
            page[r, 1] = value
            pltpu.make_async_copy(page.at[r], pages.at[table[first + r, 3]], page_sem.at[r]).start()
            keys = jnp.concatenate([pairs[r, 0], key], axis=0)
            values = jnp.concatenate([pairs[r, 1], value], axis=0)
            delta = ADAPTER_SCALE * dot(low[first + r], up[first + r], ((0,), (0,)))
            query = acc_q[rows, :] + delta.astype(BF16).astype(F32)
            for h in range(heads):
                lanes = slice(h * HEAD_WIDTH, (h + 1) * HEAD_WIDTH)
                q = rotate(query[:, lanes], cos_t, sin_t).astype(BF16)
                scores = dot(q, keys, ((1,), (1,))) * (HEAD_WIDTH**-0.5)
                scores = jnp.where(allowed, scores, -1e30)
                top = jnp.max(scores, axis=1, keepdims=True)
                weights = jnp.exp(scores - top)
                inverse = 1.0 / jnp.sum(weights, axis=1, keepdims=True)
                probs = (weights * inverse).astype(BF16)
                out = dot(probs, values)
                context[r, :, lanes] = jnp.where(live, out, 0.0).astype(BF16)
            return carry

        lax.fori_loop(0, count, request, 0)
        for r in range(count):
            pltpu.make_async_copy(page.at[r], pages.at[0], page_sem.at[r]).wait()


def block_call(first, start, count, requests, order, table, x, weights, low, up, tables, pairs, before):
    seq, width = x[0].shape[2:]
    q_width = weights[0].shape[1]
    pre = pairs[0].shape[2]
    hbm = pl.BlockSpec(memory_space=pl.ANY)
    whole = lambda a: pl.BlockSpec(a.shape, lambda k, *_: (0,) * a.ndim)
    weight = lambda a: pl.BlockSpec((width, a.shape[1]), lambda k, order, table: (order[k], 0))
    operands = [*x, *weights, low, up, *tables, *pairs, *before]
    specs = (
        [hbm] * 5
        + [weight(w) for w in weights]
        + [whole(low), whole(up)]
        + [whole(t) for t in tables]
        + [hbm] * (4 + len(before))
    )
    at = len(operands)
    aliases = {at: 0, at + 1: 1} if before else {}
    return pl.pallas_call(
        functools.partial(block_kernel, first, start, count),
        out_shape=(
            jax.ShapeDtypeStruct((requests, seq, q_width), BF16),
            jax.ShapeDtypeStruct((requests, 2, seq, HEAD_WIDTH), BF16),
        ),
        grid_spec=pltpu.PrefetchScalarGridSpec(
            num_scalar_prefetch=2,
            grid=(8,),
            in_specs=specs,
            out_specs=[pl.BlockSpec((count, seq, q_width), lambda k, *_: (first // count, 0, 0)), hbm],
            scratch_shapes=[
                pltpu.VMEM((8, count, seq, width), BF16),
                pltpu.VMEM((count * seq, q_width), F32),
                pltpu.VMEM((count * seq, 2 * HEAD_WIDTH), F32),
                pltpu.VMEM((count, 2, pre, HEAD_WIDTH), BF16),
                pltpu.VMEM((count, 2, seq, HEAD_WIDTH), BF16),
                pltpu.SemaphoreType.DMA((8,)),
                pltpu.SemaphoreType.DMA((count,)),
                pltpu.SemaphoreType.DMA((count,)),
            ],
        ),
        input_output_aliases=aliases,
        name="block",
    )(order, table, *operands)


def after(values, *others):
    return lax.optimization_barrier((tuple(values), others))[0]


def ring_rest(near):
    far = over_tensor(near[0], RING)
    return near, over_tensor(near, SWAP), far, over_tensor(far, SWAP)


def on_device(
    tokens,
    shared_prefix_tokens,
    input_norm_gain,
    query_weight,
    key_weight,
    value_weight,
    adapter_down_weight,
    adapter_up_weight,
    adapter_position,
    request_adapter,
    request_group,
    lengths,
    request_page_table,
):
    requests, seq, part = tokens.shape
    pre = shared_prefix_tokens.shape[1]
    held = adapter_up_weight.shape[0]
    column = lax.axis_index("tensor")
    place = lax.axis_index("dp")
    core = column % 2
    y = column // 2
    z_at, x_at = place // 4, place % 4

    near_y = (y + 3 + 2 * core) % 4
    cross_y = (y + 1 + 2 * core) % 4
    far_y = (y + 2) % 4
    order = jnp.stack(
        [
            column,
            column ^ 1,
            near_y * 2 + core,
            near_y * 2 + 1 - core,
            cross_y * 2 + 1 - core,
            cross_y * 2 + core,
            far_y * 2 + core,
            far_y * 2 + 1 - core,
        ]
    ).astype(jnp.int32)

    def relative(owner):
        dz, dx = (owner // 4 - z_at) % 4, (owner % 4 - x_at) % 4
        return jnp.where(core == 0, dx, dz), jnp.where(core == 0, dz, dx)

    prefix = shared_prefix_tokens.reshape(pre, part)
    prefix_other = over_tensor(prefix, SWAP)
    tokens_other = over_tensor(tokens, SWAP)
    prefix_mine = jnp.stack([prefix, prefix_other])
    prefix_near = over_tensor(prefix_mine, RING)

    square = lambda v: jnp.sum(jnp.square(v.astype(F32)), axis=-1)
    chip = square(tokens) + square(tokens_other)
    one = over_tensor(chip, BACK)
    two = over_tensor(one, BACK)
    mean = (chip + two + one + over_tensor(one, SWAP)) * (1.0 / (8 * part))
    scale = lax.rsqrt(mean + EPS).reshape(requests, 1, seq)

    prefix_rest = ring_rest(after((prefix_near,), scale)[0])
    down, up = after((adapter_down_weight, adapter_up_weight), scale)
    adapters = gather_plane(jnp.concatenate([down.transpose(0, 2, 1), up], axis=1))

    gain = input_norm_gain.astype(F32).reshape(8, 1, part)
    firsts = [sum(CHUNKS[:i]) for i in range(len(CHUNKS))]
    chunks = [
        norm_call(f, n, order[:2], tokens, tokens_other, scale, gain)
        for f, n in zip(firsts, CHUNKS)
    ]
    near = over_tensor(after(chunks[:1], prefix_rest[2])[0], RING)
    pre_cos, pre_sin = rotate_tables(0, pre)
    pair = prefix_call(
        order, prefix_mine, *prefix_rest, gain, key_weight, value_weight, pre_cos, pre_sin
    )
    pair_row = jnp.stack(over_plane(pair, 0))
    pairs = over_plane(pair_row, 1)

    ids = jnp.arange(adapter_position.shape[0])
    slots = jnp.sum(
        jnp.where(request_adapter[:, None] == ids[None, :], adapter_position[None, :], 0), axis=1
    )
    slot_1, slot_2 = relative(slots // held)
    pick = jnp.stack([slot_2, slot_1, slots % held], axis=1).astype(jnp.int32)
    part_low, up = low_call(pick, chunks, adapters)
    near = after((near,), part_low, pair_row)[0]
    chip_low = part_low + over_tensor(part_low, SWAP)
    one_low = over_tensor(chip_low, BACK)
    two_low = over_tensor(one_low, BACK)
    low = (chip_low + two_low + one_low + over_tensor(one_low, SWAP)).astype(BF16)
    far = after((over_tensor(near[0], RING),), low, *pairs)[0]
    gathered = [chunks[0], near, over_tensor(near, SWAP), far, over_tensor(far, SWAP)]
    late_near = over_tensor(after(chunks[1:], far)[0], RING)

    group_1, group_2 = relative(request_group)
    page = request_page_table.reshape(-1) - place * requests
    table = jnp.stack([group_2, group_1, lengths, page], axis=1).astype(jnp.int32)
    tables = rotate_tables(pre, seq)
    outs = ()
    for i, (chunk, start, count) in enumerate(BLOCKS):
        if i == 1:
            late_near, outs = lax.optimization_barrier((late_near, outs))
            late_far = over_tensor(late_near[0], RING)
            late_cross = over_tensor(late_near, SWAP)
        if i == 2:
            late_far, outs = lax.optimization_barrier((late_far, outs))
            late_far_cross = over_tensor(late_far, SWAP)
            gathered = [chunks[1], late_near, late_cross, late_far, late_far_cross]
        outs = block_call(
            firsts[chunk] + start,
            start,
            count,
            requests,
            order,
            table,
            gathered,
            (query_weight, key_weight, value_weight),
            low,
            up,
            tables,
            pairs,
            outs,
        )
    return outs


def solution(mesh):
    in_specs = (
        P("dp", None, "tensor"),
        P("dp", None, "tensor"),
        P(),
        P(None, "tensor"),
        P(None, "tensor"),
        P(None, "tensor"),
        P("dp", "tensor", None),
        P("dp", None, "tensor"),
        P(),
        P("dp"),
        P("dp"),
        P("dp"),
        P("dp", None),
    )
    out_specs = (P("dp", None, "tensor"), P("dp", None, None, "tensor"))
    return jax.shard_map(
        on_device, mesh=mesh, in_specs=in_specs, out_specs=out_specs, check_vma=False
    )
```

```python
import functools

import jax
import jax.numpy as jnp
import numpy as np
from jax import lax
from jax.experimental import pallas as pl
from jax.experimental.pallas import tpu as pltpu
from jax.sharding import PartitionSpec as P

HEAD_WIDTH = 128
RANK = 16
EPS = 1e-05
THETA = 500000.0
ADAPTER_SCALE = 2.0
F32 = jnp.float32
BF16 = jnp.bfloat16
CHUNKS = (4, 4)
BLOCKS = ((0, 0, 2), (0, 2, 2), (1, 0, 4))

SWAP = [(y * 2 + c, y * 2 + 1 - c) for y in range(4) for c in range(2)]
RING = [(y * 2 + c, (y + 1 - 2 * c) % 4 * 2 + c) for y in range(4) for c in range(2)]
BACK = [(y * 2 + c, (y - 1 + 2 * c) % 4 * 2 + c) for y in range(4) for c in range(2)]


def plane_shift(k, stage):
    pairs = []
    for z in range(4):
        for x in range(4):
            for t in range(8):
                along_x = (t % 2 == 0) == (stage == 0)
                to_z, to_x = (z, (x + k) % 4) if along_x else ((z + k) % 4, x)
                pairs.append(((z * 4 + x) * 8 + t, (to_z * 4 + to_x) * 8 + t))
    return pairs


def over_tensor(value, pairs):
    return lax.ppermute(value, "tensor", pairs)


def over_plane(value, stage):
    send = lambda k: lax.ppermute(value, ("dp", "tensor"), plane_shift(k, stage))
    return [value, send(-1), send(2), send(1)]


def rotate_tables(start, count):
    half = HEAD_WIDTH // 2
    freq = THETA ** (-(np.arange(half) * 2.0 / HEAD_WIDTH))
    angle = np.arange(start, start + count)[:, None] * freq[None, :]
    cosine, sine = np.cos(angle), np.sin(angle)
    return (
        np.concatenate([cosine, cosine], 1).astype(np.float32),
        np.concatenate([-sine, sine], 1).astype(np.float32),
    )


def rotate(value, cosine, sine):
    return value * cosine + pltpu.roll(value, HEAD_WIDTH // 2, 1) * sine


def dot(a, b, dims=((1,), (0,))):
    return lax.dot_general(a, b, (dims, ((), ())), preferred_element_type=F32)


def norm_kernel(place, own, other, scale, gain_own, gain_other, out):
    for r in range(own.shape[0]):
        row = jnp.broadcast_to(scale[r], (128, 128))
        eye = lax.broadcasted_iota(jnp.int32, (128, 128), 0) == lax.broadcasted_iota(
            jnp.int32, (128, 128), 1
        )
        column = jnp.sum(jnp.where(eye, row, 0.0), axis=1, keepdims=True)
        out[0, r] = (own[r].astype(F32) * column * gain_own[0]).astype(BF16)
        out[1, r] = (other[r].astype(F32) * column * gain_other[0]).astype(BF16)


def norm_call(first, count, gain_ids, own, other, scale, gain):
    _, seq, part = own.shape
    rows = lambda i, ids: (first + i, 0, 0)
    return pl.pallas_call(
        norm_kernel,
        out_shape=jax.ShapeDtypeStruct((2, count, seq, part), BF16),
        grid_spec=pltpu.PrefetchScalarGridSpec(
            num_scalar_prefetch=1,
            grid=(count,),
            in_specs=[
                pl.BlockSpec((1, seq, part), rows),
                pl.BlockSpec((1, seq, part), rows),
                pl.BlockSpec((1, 1, seq), rows),
                pl.BlockSpec((1, 1, part), lambda i, ids: (ids[0], 0, 0)),
                pl.BlockSpec((1, 1, part), lambda i, ids: (ids[1], 0, 0)),
            ],
            out_specs=pl.BlockSpec((2, 1, seq, part), lambda i, ids: (0, i, 0, 0)),
        ),
        name="norm",
    )(gain_ids, own, other, scale, gain, gain)


def prefix_kernel(order, mine, near, cross, far, far_cross, gain, kw, vw, cosine, sine, out):
    width = mine.shape[-1]
    pieces = [mine[0], mine[1], near[0], near[1], cross[0], cross[1], far[...], far_cross[...]]
    total = jnp.zeros((mine.shape[1], 1), F32)
    for piece in pieces:
        value = piece.astype(F32)
        total = total + jnp.sum(value * value, axis=1, keepdims=True)
    scale = lax.rsqrt(total * (1.0 / (8 * width)) + EPS)
    acc = jnp.zeros((mine.shape[1], 2 * HEAD_WIDTH), F32)
    for i, piece in enumerate(pieces):
        block = order[i]
        at = pl.ds(pl.multiple_of(block * width, width), width)
        weight = jnp.concatenate([kw[at, :], vw[at, :]], axis=1)
        normed = (piece.astype(F32) * scale * gain[block]).astype(BF16)
        acc = acc + dot(normed, weight)
    out[0] = rotate(acc[:, :HEAD_WIDTH], cosine[...], sine[...]).astype(BF16)
    out[1] = acc[:, HEAD_WIDTH:].astype(BF16)


def prefix_call(order, mine, near, cross, far, far_cross, gain, kw, vw, cosine, sine):
    rows = mine.shape[1]
    full = pl.BlockSpec(memory_space=pltpu.VMEM)
    return pl.pallas_call(
        prefix_kernel,
        out_shape=jax.ShapeDtypeStruct((2, rows, HEAD_WIDTH), BF16),
        in_specs=[pl.BlockSpec(memory_space=pltpu.SMEM)] + [full] * 10,
        out_specs=full,
        name="prefix",
    )(order, mine, near, cross, far, far_cross, gain, kw, vw, cosine, sine)


def pick_copies(sources, select, first, second, target, sem, act):
    for j, source in enumerate(sources):

        @pl.when(select == j)
        def _(source=source):
            act(pltpu.make_async_copy(source.at[first] if second is None else source.at[first, second], target, sem))


def low_kernel(pick, x0, x1, a0, a1, a2, a3, part, up, held, sems):
    for r in range(held.shape[0]):
        pick_copies(
            (a0, a1, a2, a3), pick[r, 0], pick[r, 1], pick[r, 2], held.at[r], sems.at[r], lambda c: c.start()
        )
    r = 0
    for x in (x0, x1):
        for i in range(x.shape[1]):
            pltpu.make_async_copy(a0.at[0, 0], held.at[r], sems.at[r]).wait()
            part[r] = dot(held[r, :RANK], x[0, i], ((1,), (1,)))
            up[r] = held[r, RANK:]
            r += 1


def low_call(pick, chunks, adapters):
    requests = pick.shape[0]
    seq, part = chunks[0].shape[2:]
    full = pl.BlockSpec(memory_space=pltpu.VMEM)
    some = [pl.BlockSpec((1,) + c.shape[1:], lambda i, *_: (0, 0, 0, 0)) for c in chunks]
    return pl.pallas_call(
        low_kernel,
        out_shape=(
            jax.ShapeDtypeStruct((requests, RANK, seq), F32),
            jax.ShapeDtypeStruct((requests, RANK, part), BF16),
        ),
        grid_spec=pltpu.PrefetchScalarGridSpec(
            num_scalar_prefetch=1,
            grid=(1,),
            in_specs=some + [pl.BlockSpec(memory_space=pl.ANY)] * 4,
            out_specs=[
                pl.BlockSpec((requests, RANK, seq), lambda i, *_: (0, 0, 0)),
                pl.BlockSpec((requests, RANK, part), lambda i, *_: (0, 0, 0)),
            ],
            scratch_shapes=[
                pltpu.VMEM((requests, 2 * RANK, part), BF16),
                pltpu.SemaphoreType.DMA((requests,)),
            ],
        ),
        name="low",
    )(pick, *chunks, *adapters)


def block_kernel(
    first,
    start,
    count,
    order,
    table,
    mine,
    near,
    cross,
    far,
    far_cross,
    qw,
    kw,
    vw,
    low,
    up,
    cosine,
    sine,
    p0,
    p1,
    p2,
    p3,
    *rest,
):
    context, pages, xs, acc_q, acc_kv, pairs, page, x_sem, pair_sem, page_sem = rest[-10:]
    k = pl.program_id(0)
    seq, width = xs.shape[2:]
    pre = pairs.shape[2]
    sources = [mine.at[0], mine.at[1], near.at[0], near.at[1], cross.at[0], cross.at[1], far, far_cross]

    @pl.when(k == 0)
    def _():
        for i, source in enumerate(sources):
            pltpu.make_async_copy(source.at[start : start + count], xs.at[i], x_sem.at[i]).start()
        for r in range(count):
            pick_copies(
                (p0, p1, p2, p3),
                table[first + r, 0],
                table[first + r, 1],
                None,
                pairs.at[r],
                pair_sem.at[r],
                lambda c: c.start(),
            )

    pltpu.make_async_copy(far.at[start : start + count], xs.at[k], x_sem.at[k]).wait()
    x = xs[k].reshape(count * seq, width)
    part_q = dot(x, qw[...])
    part_kv = dot(x, jnp.concatenate([kw[...], vw[...]], axis=1))

    @pl.when(k == 0)
    def _():
        acc_q[...] = part_q
        acc_kv[...] = part_kv

    @pl.when(k > 0)
    def _():
        acc_q[...] += part_q
        acc_kv[...] += part_kv

    @pl.when(k == pl.num_programs(0) - 1)
    def _():
        heads = acc_q.shape[1] // HEAD_WIDTH
        cos_t, sin_t = cosine[...], sine[...]
        token = lax.broadcasted_iota(jnp.int32, (seq, HEAD_WIDTH), 0)
        causal = lax.broadcasted_iota(jnp.int32, (seq, seq), 1) <= lax.broadcasted_iota(
            jnp.int32, (seq, seq), 0
        )
        allowed = jnp.concatenate([jnp.ones((seq, pre), jnp.bool_), causal], axis=1)

        def request(r, carry):
            pltpu.make_async_copy(p0.at[0], pairs.at[r], pair_sem.at[r]).wait()
            live = token < table[first + r, 2]
            rows = pl.ds(pl.multiple_of(r * seq, seq), seq)
            key = rotate(acc_kv[rows, :HEAD_WIDTH], cos_t, sin_t)
            key = jnp.where(live, key, 0.0).astype(BF16)
            value = jnp.where(live, acc_kv[rows, HEAD_WIDTH:], 0.0).astype(BF16)
            page[r, 0] = key
            page[r, 1] = value
            pltpu.make_async_copy(page.at[r], pages.at[table[first + r, 3]], page_sem.at[r]).start()
            keys = jnp.concatenate([pairs[r, 0], key], axis=0)
            values = jnp.concatenate([pairs[r, 1], value], axis=0)
            delta = ADAPTER_SCALE * dot(low[first + r], up[first + r], ((0,), (0,)))
            query = acc_q[rows, :] + delta.astype(BF16).astype(F32)
            for h in range(heads):
                lanes = slice(h * HEAD_WIDTH, (h + 1) * HEAD_WIDTH)
                q = rotate(query[:, lanes], cos_t, sin_t).astype(BF16)
                scores = dot(q, keys, ((1,), (1,))) * (HEAD_WIDTH**-0.5)
                scores = jnp.where(allowed, scores, -1e30)
                top = jnp.max(scores, axis=1, keepdims=True)
                weights = jnp.exp(scores - top)
                inverse = 1.0 / jnp.sum(weights, axis=1, keepdims=True)
                probs = (weights * inverse).astype(BF16)
                out = dot(probs, values)
                context[r, :, lanes] = jnp.where(live, out, 0.0).astype(BF16)
            return carry

        lax.fori_loop(0, count, request, 0)
        for r in range(count):
            pltpu.make_async_copy(page.at[r], pages.at[0], page_sem.at[r]).wait()


def block_call(first, start, count, requests, order, table, x, weights, low, up, tables, pairs, before):
    seq, width = x[0].shape[2:]
    q_width = weights[0].shape[1]
    pre = pairs[0].shape[2]
    hbm = pl.BlockSpec(memory_space=pl.ANY)
    whole = lambda a: pl.BlockSpec(a.shape, lambda k, *_: (0,) * a.ndim)
    weight = lambda a: pl.BlockSpec((width, a.shape[1]), lambda k, order, table: (order[k], 0))
    operands = [*x, *weights, low, up, *tables, *pairs, *before]
    specs = (
        [hbm] * 5
        + [weight(w) for w in weights]
        + [whole(low), whole(up)]
        + [whole(t) for t in tables]
        + [hbm] * (4 + len(before))
    )
    at = len(operands)
    aliases = {at: 0, at + 1: 1} if before else {}
    return pl.pallas_call(
        functools.partial(block_kernel, first, start, count),
        out_shape=(
            jax.ShapeDtypeStruct((requests, seq, q_width), BF16),
            jax.ShapeDtypeStruct((requests, 2, seq, HEAD_WIDTH), BF16),
        ),
        grid_spec=pltpu.PrefetchScalarGridSpec(
            num_scalar_prefetch=2,
            grid=(8,),
            in_specs=specs,
            out_specs=[pl.BlockSpec((count, seq, q_width), lambda k, *_: (first // count, 0, 0)), hbm],
            scratch_shapes=[
                pltpu.VMEM((8, count, seq, width), BF16),
                pltpu.VMEM((count * seq, q_width), F32),
                pltpu.VMEM((count * seq, 2 * HEAD_WIDTH), F32),
                pltpu.VMEM((count, 2, pre, HEAD_WIDTH), BF16),
                pltpu.VMEM((count, 2, seq, HEAD_WIDTH), BF16),
                pltpu.SemaphoreType.DMA((8,)),
                pltpu.SemaphoreType.DMA((count,)),
                pltpu.SemaphoreType.DMA((count,)),
            ],
        ),
        input_output_aliases=aliases,
        name="block",
    )(order, table, *operands)


def after(values, *others):
    return lax.optimization_barrier((tuple(values), others))[0]


def ring_rest(near):
    far = over_tensor(near[0], RING)
    return near, over_tensor(near, SWAP), far, over_tensor(far, SWAP)


def on_device(
    tokens,
    shared_prefix_tokens,
    input_norm_gain,
    query_weight,
    key_weight,
    value_weight,
    adapter_down_weight,
    adapter_up_weight,
    adapter_position,
    request_adapter,
    request_group,
    lengths,
    request_page_table,
):
    requests, seq, part = tokens.shape
    pre = shared_prefix_tokens.shape[1]
    held = adapter_up_weight.shape[0]
    column = lax.axis_index("tensor")
    place = lax.axis_index("dp")
    core = column % 2
    y = column // 2
    z_at, x_at = place // 4, place % 4

    near_y = (y + 3 + 2 * core) % 4
    cross_y = (y + 1 + 2 * core) % 4
    far_y = (y + 2) % 4
    order = jnp.stack(
        [
            column,
            column ^ 1,
            near_y * 2 + core,
            near_y * 2 + 1 - core,
            cross_y * 2 + 1 - core,
            cross_y * 2 + core,
            far_y * 2 + core,
            far_y * 2 + 1 - core,
        ]
    ).astype(jnp.int32)

    def relative(owner):
        dz, dx = (owner // 4 - z_at) % 4, (owner % 4 - x_at) % 4
        return jnp.where(core == 0, dx, dz), jnp.where(core == 0, dz, dx)

    prefix = shared_prefix_tokens.reshape(pre, part)
    prefix_other = over_tensor(prefix, SWAP)
    tokens_other = over_tensor(tokens, SWAP)
    adapter_row = over_plane(
        jnp.concatenate([adapter_down_weight.transpose(0, 2, 1), adapter_up_weight], axis=1), 0
    )
    prefix_mine = jnp.stack([prefix, prefix_other])
    prefix_near = over_tensor(prefix_mine, RING)

    square = lambda v: jnp.sum(jnp.square(v.astype(F32)), axis=-1)
    chip = square(tokens) + square(tokens_other)
    adapter_row = jnp.stack(after(adapter_row, chip))
    adapters = over_plane(adapter_row, 1)
    one = after((over_tensor(chip, BACK),), adapter_row)[0]
    two = over_tensor(one, BACK)
    mean = (chip + two + one + over_tensor(one, SWAP)) * (1.0 / (8 * part))
    scale = lax.rsqrt(mean + EPS).reshape(requests, 1, seq)

    prefix_rest = ring_rest(after((prefix_near,), scale)[0])
    gain = input_norm_gain.astype(F32).reshape(8, 1, part)
    firsts = [sum(CHUNKS[:i]) for i in range(len(CHUNKS))]
    chunks = [
        norm_call(f, n, order[:2], tokens, tokens_other, scale, gain)
        for f, n in zip(firsts, CHUNKS)
    ]
    near = over_tensor(after(chunks[:1], prefix_rest[2], adapters[1], adapters[3])[0], RING)
    pre_cos, pre_sin = rotate_tables(0, pre)
    pair = prefix_call(
        order, prefix_mine, *prefix_rest, gain, key_weight, value_weight, pre_cos, pre_sin
    )
    pair_row = jnp.stack(over_plane(pair, 0))
    pairs = over_plane(pair_row, 1)

    ids = jnp.arange(adapter_position.shape[0])
    slots = jnp.sum(
        jnp.where(request_adapter[:, None] == ids[None, :], adapter_position[None, :], 0), axis=1
    )
    slot_1, slot_2 = relative(slots // held)
    pick = jnp.stack([slot_2, slot_1, slots % held], axis=1).astype(jnp.int32)
    part_low, up = low_call(pick, chunks, adapters)
    near = after((near,), part_low, pair_row)[0]
    chip_low = part_low + over_tensor(part_low, SWAP)
    one_low = over_tensor(chip_low, BACK)
    two_low = over_tensor(one_low, BACK)
    low = (chip_low + two_low + one_low + over_tensor(one_low, SWAP)).astype(BF16)
    far = after((over_tensor(near[0], RING),), low, *pairs)[0]
    gathered = [chunks[0], near, over_tensor(near, SWAP), far, over_tensor(far, SWAP)]
    late_near = over_tensor(after(chunks[1:], far)[0], RING)

    group_1, group_2 = relative(request_group)
    page = request_page_table.reshape(-1) - place * requests
    table = jnp.stack([group_2, group_1, lengths, page], axis=1).astype(jnp.int32)
    tables = rotate_tables(pre, seq)
    outs = ()
    for i, (chunk, start, count) in enumerate(BLOCKS):
        if i == 1:
            late_near, outs = lax.optimization_barrier((late_near, outs))
            late_far = over_tensor(late_near[0], RING)
            late_cross = over_tensor(late_near, SWAP)
        if i == 2:
            late_far, outs = lax.optimization_barrier((late_far, outs))
            late_far_cross = over_tensor(late_far, SWAP)
            gathered = [chunks[1], late_near, late_cross, late_far, late_far_cross]
        outs = block_call(
            firsts[chunk] + start,
            start,
            count,
            requests,
            order,
            table,
            gathered,
            (query_weight, key_weight, value_weight),
            low,
            up,
            tables,
            pairs,
            outs,
        )
    return outs


def solution(mesh):
    in_specs = (
        P("dp", None, "tensor"),
        P("dp", None, "tensor"),
        P(),
        P(None, "tensor"),
        P(None, "tensor"),
        P(None, "tensor"),
        P("dp", "tensor", None),
        P("dp", None, "tensor"),
        P(),
        P("dp"),
        P("dp"),
        P("dp"),
        P("dp", None),
    )
    out_specs = (P("dp", None, "tensor"), P("dp", None, None, "tensor"))
    return jax.shard_map(
        on_device, mesh=mesh, in_specs=in_specs, out_specs=out_specs, check_vma=False
    )
```

```python
import functools

import jax
import jax.numpy as jnp
import numpy as np
from jax import lax
from jax.experimental import pallas as pl
from jax.experimental.pallas import tpu as pltpu
from jax.sharding import PartitionSpec as P

HEAD_WIDTH = 128
RANK = 16
EPS = 1e-05
THETA = 500000.0
ADAPTER_SCALE = 2.0
F32 = jnp.float32
BF16 = jnp.bfloat16
CHUNKS = (4, 4)
BLOCKS = ((0, 0, 4), (1, 0, 4))

SWAP = [(y * 2 + c, y * 2 + 1 - c) for y in range(4) for c in range(2)]
RING = [(y * 2 + c, (y + 1 - 2 * c) % 4 * 2 + c) for y in range(4) for c in range(2)]
BACK = [(y * 2 + c, (y - 1 + 2 * c) % 4 * 2 + c) for y in range(4) for c in range(2)]


def plane_shift(k, stage):
    pairs = []
    for z in range(4):
        for x in range(4):
            for t in range(8):
                along_x = (t % 2 == 0) == (stage == 0)
                to_z, to_x = (z, (x + k) % 4) if along_x else ((z + k) % 4, x)
                pairs.append(((z * 4 + x) * 8 + t, (to_z * 4 + to_x) * 8 + t))
    return pairs


def over_tensor(value, pairs):
    return lax.ppermute(value, "tensor", pairs)


def over_plane(value, stage):
    send = lambda k: lax.ppermute(value, ("dp", "tensor"), plane_shift(k, stage))
    return [value, send(-1), send(2), send(1)]


def rotate_tables(start, count):
    half = HEAD_WIDTH // 2
    freq = THETA ** (-(np.arange(half) * 2.0 / HEAD_WIDTH))
    angle = np.arange(start, start + count)[:, None] * freq[None, :]
    cosine, sine = np.cos(angle), np.sin(angle)
    return (
        np.concatenate([cosine, cosine], 1).astype(np.float32),
        np.concatenate([-sine, sine], 1).astype(np.float32),
    )


def rotate(value, cosine, sine):
    return value * cosine + pltpu.roll(value, HEAD_WIDTH // 2, 1) * sine


def dot(a, b, dims=((1,), (0,))):
    return lax.dot_general(a, b, (dims, ((), ())), preferred_element_type=F32)


def norm_kernel(place, own, other, scale, gain_own, gain_other, out):
    for r in range(own.shape[0]):
        row = jnp.broadcast_to(scale[r], (128, 128))
        eye = lax.broadcasted_iota(jnp.int32, (128, 128), 0) == lax.broadcasted_iota(
            jnp.int32, (128, 128), 1
        )
        column = jnp.sum(jnp.where(eye, row, 0.0), axis=1, keepdims=True)
        out[0, r] = (own[r].astype(F32) * column * gain_own[0]).astype(BF16)
        out[1, r] = (other[r].astype(F32) * column * gain_other[0]).astype(BF16)


def norm_call(first, count, gain_ids, own, other, scale, gain):
    _, seq, part = own.shape
    rows = lambda i, ids: (first + i, 0, 0)
    return pl.pallas_call(
        norm_kernel,
        out_shape=jax.ShapeDtypeStruct((2, count, seq, part), BF16),
        grid_spec=pltpu.PrefetchScalarGridSpec(
            num_scalar_prefetch=1,
            grid=(count,),
            in_specs=[
                pl.BlockSpec((1, seq, part), rows),
                pl.BlockSpec((1, seq, part), rows),
                pl.BlockSpec((1, 1, seq), rows),
                pl.BlockSpec((1, 1, part), lambda i, ids: (ids[0], 0, 0)),
                pl.BlockSpec((1, 1, part), lambda i, ids: (ids[1], 0, 0)),
            ],
            out_specs=pl.BlockSpec((2, 1, seq, part), lambda i, ids: (0, i, 0, 0)),
        ),
        name="norm",
    )(gain_ids, own, other, scale, gain, gain)


def prefix_kernel(order, mine, near, cross, far, far_cross, gain, kw, vw, cosine, sine, out):
    width = mine.shape[-1]
    pieces = [mine[0], mine[1], near[0], near[1], cross[0], cross[1], far[...], far_cross[...]]
    total = jnp.zeros((mine.shape[1], 1), F32)
    for piece in pieces:
        value = piece.astype(F32)
        total = total + jnp.sum(value * value, axis=1, keepdims=True)
    scale = lax.rsqrt(total * (1.0 / (8 * width)) + EPS)
    acc = jnp.zeros((mine.shape[1], 2 * HEAD_WIDTH), F32)
    for i, piece in enumerate(pieces):
        block = order[i]
        at = pl.ds(pl.multiple_of(block * width, width), width)
        weight = jnp.concatenate([kw[at, :], vw[at, :]], axis=1)
        normed = (piece.astype(F32) * scale * gain[block]).astype(BF16)
        acc = acc + dot(normed, weight)
    out[0] = rotate(acc[:, :HEAD_WIDTH], cosine[...], sine[...]).astype(BF16)
    out[1] = acc[:, HEAD_WIDTH:].astype(BF16)


def prefix_call(order, mine, near, cross, far, far_cross, gain, kw, vw, cosine, sine):
    rows = mine.shape[1]
    full = pl.BlockSpec(memory_space=pltpu.VMEM)
    return pl.pallas_call(
        prefix_kernel,
        out_shape=jax.ShapeDtypeStruct((2, rows, HEAD_WIDTH), BF16),
        in_specs=[pl.BlockSpec(memory_space=pltpu.SMEM)] + [full] * 10,
        out_specs=full,
        name="prefix",
    )(order, mine, near, cross, far, far_cross, gain, kw, vw, cosine, sine)


def pick_copies(sources, select, first, second, target, sem, act):
    for j, source in enumerate(sources):

        @pl.when(select == j)
        def _(source=source):
            act(pltpu.make_async_copy(source.at[first] if second is None else source.at[first, second], target, sem))


def low_kernel(pick, x0, x1, a0, a1, a2, a3, part, up, held, sems):
    for r in range(held.shape[0]):
        pick_copies(
            (a0, a1, a2, a3), pick[r, 0], pick[r, 1], pick[r, 2], held.at[r], sems.at[r], lambda c: c.start()
        )
    r = 0
    for x in (x0, x1):
        for i in range(x.shape[1]):
            pltpu.make_async_copy(a0.at[0, 0], held.at[r], sems.at[r]).wait()
            part[r] = dot(held[r, :RANK], x[0, i], ((1,), (1,)))
            up[r] = held[r, RANK:]
            r += 1


def low_call(pick, chunks, adapters):
    requests = pick.shape[0]
    seq, part = chunks[0].shape[2:]
    full = pl.BlockSpec(memory_space=pltpu.VMEM)
    some = [pl.BlockSpec((1,) + c.shape[1:], lambda i, *_: (0, 0, 0, 0)) for c in chunks]
    return pl.pallas_call(
        low_kernel,
        out_shape=(
            jax.ShapeDtypeStruct((requests, RANK, seq), F32),
            jax.ShapeDtypeStruct((requests, RANK, part), BF16),
        ),
        grid_spec=pltpu.PrefetchScalarGridSpec(
            num_scalar_prefetch=1,
            grid=(1,),
            in_specs=some + [pl.BlockSpec(memory_space=pl.ANY)] * 4,
            out_specs=[
                pl.BlockSpec((requests, RANK, seq), lambda i, *_: (0, 0, 0)),
                pl.BlockSpec((requests, RANK, part), lambda i, *_: (0, 0, 0)),
            ],
            scratch_shapes=[
                pltpu.VMEM((requests, 2 * RANK, part), BF16),
                pltpu.SemaphoreType.DMA((requests,)),
            ],
        ),
        name="low",
    )(pick, *chunks, *adapters)


def block_kernel(
    first,
    start,
    count,
    order,
    table,
    mine,
    near,
    cross,
    far,
    far_cross,
    qw,
    kw,
    vw,
    low,
    up,
    cosine,
    sine,
    p0,
    p1,
    p2,
    p3,
    *rest,
):
    context, pages, xs, acc_q, acc_kv, pairs, page, x_sem, pair_sem, page_sem = rest[-10:]
    k = pl.program_id(0)
    seq, width = xs.shape[2:]
    pre = pairs.shape[2]
    sources = [mine.at[0], mine.at[1], near.at[0], near.at[1], cross.at[0], cross.at[1], far, far_cross]

    @pl.when(k == 0)
    def _():
        for i, source in enumerate(sources):
            pltpu.make_async_copy(source.at[start : start + count], xs.at[i], x_sem.at[i]).start()
        for r in range(count):
            pick_copies(
                (p0, p1, p2, p3),
                table[first + r, 0],
                table[first + r, 1],
                None,
                pairs.at[r],
                pair_sem.at[r],
                lambda c: c.start(),
            )

    pltpu.make_async_copy(far.at[start : start + count], xs.at[k], x_sem.at[k]).wait()
    x = xs[k].reshape(count * seq, width)
    part_q = dot(x, qw[...])
    part_kv = dot(x, jnp.concatenate([kw[...], vw[...]], axis=1))

    @pl.when(k == 0)
    def _():
        acc_q[...] = part_q
        acc_kv[...] = part_kv

    @pl.when(k > 0)
    def _():
        acc_q[...] += part_q
        acc_kv[...] += part_kv

    @pl.when(k == pl.num_programs(0) - 1)
    def _():
        heads = acc_q.shape[1] // HEAD_WIDTH
        cos_t, sin_t = cosine[...], sine[...]
        token = lax.broadcasted_iota(jnp.int32, (seq, HEAD_WIDTH), 0)
        causal = lax.broadcasted_iota(jnp.int32, (seq, seq), 1) <= lax.broadcasted_iota(
            jnp.int32, (seq, seq), 0
        )
        allowed = jnp.concatenate([jnp.ones((seq, pre), jnp.bool_), causal], axis=1)

        def request(r, carry):
            pltpu.make_async_copy(p0.at[0], pairs.at[r], pair_sem.at[r]).wait()
            live = token < table[first + r, 2]
            rows = pl.ds(pl.multiple_of(r * seq, seq), seq)
            key = rotate(acc_kv[rows, :HEAD_WIDTH], cos_t, sin_t)
            key = jnp.where(live, key, 0.0).astype(BF16)
            value = jnp.where(live, acc_kv[rows, HEAD_WIDTH:], 0.0).astype(BF16)
            page[r, 0] = key
            page[r, 1] = value
            pltpu.make_async_copy(page.at[r], pages.at[table[first + r, 3]], page_sem.at[r]).start()
            keys = jnp.concatenate([pairs[r, 0], key], axis=0)
            values = jnp.concatenate([pairs[r, 1], value], axis=0)
            delta = ADAPTER_SCALE * dot(low[first + r], up[first + r], ((0,), (0,)))
            query = acc_q[rows, :] + delta.astype(BF16).astype(F32)
            for h in range(heads):
                lanes = slice(h * HEAD_WIDTH, (h + 1) * HEAD_WIDTH)
                q = rotate(query[:, lanes], cos_t, sin_t).astype(BF16)
                scores = dot(q, keys, ((1,), (1,))) * (HEAD_WIDTH**-0.5)
                scores = jnp.where(allowed, scores, -1e30)
                top = jnp.max(scores, axis=1, keepdims=True)
                weights = jnp.exp(scores - top)
                inverse = 1.0 / jnp.sum(weights, axis=1, keepdims=True)
                probs = (weights * inverse).astype(BF16)
                out = dot(probs, values)
                context[r, :, lanes] = jnp.where(live, out, 0.0).astype(BF16)
            return carry

        lax.fori_loop(0, count, request, 0)
        for r in range(count):
            pltpu.make_async_copy(page.at[r], pages.at[0], page_sem.at[r]).wait()


def block_call(first, start, count, requests, order, table, x, weights, low, up, tables, pairs, before):
    seq, width = x[0].shape[2:]
    q_width = weights[0].shape[1]
    pre = pairs[0].shape[2]
    hbm = pl.BlockSpec(memory_space=pl.ANY)
    whole = lambda a: pl.BlockSpec(a.shape, lambda k, *_: (0,) * a.ndim)
    weight = lambda a: pl.BlockSpec((width, a.shape[1]), lambda k, order, table: (order[k], 0))
    operands = [*x, *weights, low, up, *tables, *pairs, *before]
    specs = (
        [hbm] * 5
        + [weight(w) for w in weights]
        + [whole(low), whole(up)]
        + [whole(t) for t in tables]
        + [hbm] * (4 + len(before))
    )
    at = len(operands)
    aliases = {at: 0, at + 1: 1} if before else {}
    return pl.pallas_call(
        functools.partial(block_kernel, first, start, count),
        out_shape=(
            jax.ShapeDtypeStruct((requests, seq, q_width), BF16),
            jax.ShapeDtypeStruct((requests, 2, seq, HEAD_WIDTH), BF16),
        ),
        grid_spec=pltpu.PrefetchScalarGridSpec(
            num_scalar_prefetch=2,
            grid=(8,),
            in_specs=specs,
            out_specs=[pl.BlockSpec((count, seq, q_width), lambda k, *_: (first // count, 0, 0)), hbm],
            scratch_shapes=[
                pltpu.VMEM((8, count, seq, width), BF16),
                pltpu.VMEM((count * seq, q_width), F32),
                pltpu.VMEM((count * seq, 2 * HEAD_WIDTH), F32),
                pltpu.VMEM((count, 2, pre, HEAD_WIDTH), BF16),
                pltpu.VMEM((count, 2, seq, HEAD_WIDTH), BF16),
                pltpu.SemaphoreType.DMA((8,)),
                pltpu.SemaphoreType.DMA((count,)),
                pltpu.SemaphoreType.DMA((count,)),
            ],
        ),
        input_output_aliases=aliases,
        name="block",
    )(order, table, *operands)


def after(values, *others):
    return lax.optimization_barrier((tuple(values), others))[0]


def ring_rest(near):
    far = over_tensor(near[0], RING)
    return near, over_tensor(near, SWAP), far, over_tensor(far, SWAP)


def on_device(
    tokens,
    shared_prefix_tokens,
    input_norm_gain,
    query_weight,
    key_weight,
    value_weight,
    adapter_down_weight,
    adapter_up_weight,
    adapter_position,
    request_adapter,
    request_group,
    lengths,
    request_page_table,
):
    requests, seq, part = tokens.shape
    pre = shared_prefix_tokens.shape[1]
    held = adapter_up_weight.shape[0]
    column = lax.axis_index("tensor")
    place = lax.axis_index("dp")
    core = column % 2
    y = column // 2
    z_at, x_at = place // 4, place % 4

    near_y = (y + 3 + 2 * core) % 4
    cross_y = (y + 1 + 2 * core) % 4
    far_y = (y + 2) % 4
    order = jnp.stack(
        [
            column,
            column ^ 1,
            near_y * 2 + core,
            near_y * 2 + 1 - core,
            cross_y * 2 + 1 - core,
            cross_y * 2 + core,
            far_y * 2 + core,
            far_y * 2 + 1 - core,
        ]
    ).astype(jnp.int32)

    def relative(owner):
        dz, dx = (owner // 4 - z_at) % 4, (owner % 4 - x_at) % 4
        return jnp.where(core == 0, dx, dz), jnp.where(core == 0, dz, dx)

    prefix = shared_prefix_tokens.reshape(pre, part)
    prefix_other = over_tensor(prefix, SWAP)
    tokens_other = over_tensor(tokens, SWAP)
    adapter_row = over_plane(
        jnp.concatenate([adapter_down_weight.transpose(0, 2, 1), adapter_up_weight], axis=1), 0
    )
    prefix_mine = jnp.stack([prefix, prefix_other])
    prefix_near = over_tensor(prefix_mine, RING)

    square = lambda v: jnp.sum(jnp.square(v.astype(F32)), axis=-1)
    chip = square(tokens) + square(tokens_other)
    adapter_row = jnp.stack(after(adapter_row, chip))
    adapters = over_plane(adapter_row, 1)
    one = after((over_tensor(chip, BACK),), adapter_row)[0]
    two = over_tensor(one, BACK)
    mean = (chip + two + one + over_tensor(one, SWAP)) * (1.0 / (8 * part))
    scale = lax.rsqrt(mean + EPS).reshape(requests, 1, seq)

    prefix_rest = ring_rest(after((prefix_near,), scale)[0])
    gain = input_norm_gain.astype(F32).reshape(8, 1, part)
    firsts = [sum(CHUNKS[:i]) for i in range(len(CHUNKS))]
    chunks = [
        norm_call(f, n, order[:2], tokens, tokens_other, scale, gain)
        for f, n in zip(firsts, CHUNKS)
    ]
    near = over_tensor(after(chunks[:1], prefix_rest[2], adapters[1], adapters[3])[0], RING)
    pre_cos, pre_sin = rotate_tables(0, pre)
    pair = prefix_call(
        order, prefix_mine, *prefix_rest, gain, key_weight, value_weight, pre_cos, pre_sin
    )
    pair_row = jnp.stack(over_plane(pair, 0))
    pairs = over_plane(pair_row, 1)

    ids = jnp.arange(adapter_position.shape[0])
    slots = jnp.sum(
        jnp.where(request_adapter[:, None] == ids[None, :], adapter_position[None, :], 0), axis=1
    )
    slot_1, slot_2 = relative(slots // held)
    pick = jnp.stack([slot_2, slot_1, slots % held], axis=1).astype(jnp.int32)
    part_low, up = low_call(pick, chunks, adapters)
    near = after((near,), part_low, pair_row)[0]
    chip_low = part_low + over_tensor(part_low, SWAP)
    one_low = over_tensor(chip_low, BACK)
    two_low = over_tensor(one_low, BACK)
    low = (chip_low + two_low + one_low + over_tensor(one_low, SWAP)).astype(BF16)
    far = after((over_tensor(near[0], RING),), low, *pairs)[0]
    gathered = [chunks[0], near, over_tensor(near, SWAP), far, over_tensor(far, SWAP)]
    late_near = over_tensor(after(chunks[1:], one_low, near)[0], RING)

    group_1, group_2 = relative(request_group)
    page = request_page_table.reshape(-1) - place * requests
    table = jnp.stack([group_2, group_1, lengths, page], axis=1).astype(jnp.int32)
    tables = rotate_tables(pre, seq)
    late_far = over_tensor(late_near[0], RING)
    late_cross = over_tensor(late_near, SWAP)
    outs = ()
    for i, (chunk, start, count) in enumerate(BLOCKS):
        if i == 1:
            late_far, outs = lax.optimization_barrier((late_far, outs))
            late_far_cross = over_tensor(late_far, SWAP)
            gathered = [chunks[1], late_near, late_cross, late_far, late_far_cross]
        outs = block_call(
            firsts[chunk] + start,
            start,
            count,
            requests,
            order,
            table,
            gathered,
            (query_weight, key_weight, value_weight),
            low,
            up,
            tables,
            pairs,
            outs,
        )
    return outs


def solution(mesh):
    in_specs = (
        P("dp", None, "tensor"),
        P("dp", None, "tensor"),
        P(),
        P(None, "tensor"),
        P(None, "tensor"),
        P(None, "tensor"),
        P("dp", "tensor", None),
        P("dp", None, "tensor"),
        P(),
        P("dp"),
        P("dp"),
        P("dp"),
        P("dp", None),
    )
    out_specs = (P("dp", None, "tensor"), P("dp", None, None, "tensor"))
    return jax.shard_map(
        on_device, mesh=mesh, in_specs=in_specs, out_specs=out_specs, check_vma=False
    )
```
